128 devices in a mesh: tile: 32 (over z, y, x_hi), lev: 4 (over x_lo, core).
Axes of the slice: x: 4 (x_hi: 2, x_lo: 2; x = x_hi * 2 + x_lo), y: 4, z: 4, core: 2. Of those that a mesh axis runs over, the one named last changes fastest.
Arguments:
- thermal_state: float32 [128, 131072], P('lev', 'tile'), may hold values from 0.5 to 1.5
- humidity_loading: float32 [128, 131072], P('lev', 'tile'), may hold values from 0 to 1
- interface_mixing_strength: float32 [128, 131072], P('lev', 'tile'), may hold values from 1 to 30
- passive_species: bfloat16 [8, 128, 131072], P(None, 'lev', 'tile'), may hold values from -6 to 6
- terrain_height: float32 [131072], P('tile'), may hold values from -6 to 6
- log_bottom_stress: float32 [131072], P('tile'), may hold values from -3 to 3
- side_length_share: float32 [6, 131072], P(None, 'tile'), may hold values from 0.5 to 2
- adjacency_table: int32 [6, 131072], P(None, 'tile'), may hold values from 0 to 6143, as said below
Outputs:
- gravity_height: float32 [128, 131072], P('lev', 'tile')
- force_divergence: float32 [128, 131072], P('lev', 'tile')
- new_tracers: float32 [8, 128, 131072], P(None, 'lev', 'tile')
The draws below stay inside these ranges and needn't reach their ends.
Inputs may be any that keep to these rules, and one draw needn't show every extreme that they name: adjacency_table[m, c] is the position of column c's m-th neighbour among its tile's columns extended by 1024 columns of each adjacent tile on both sides (the band closes on itself); it lies within 1024 positions of the column's own position and is never the column itself.
All inputs are finite; a program needn't handle non-finite values.
Results may differ from the reference program's by a relative error of at most 0.00045.
Values may be sent and summed in bfloat16 or wider, within the bound.
A program may use at most 128 MiB of HBM per device.

```python
import math
import jax
import jax.numpy as jnp
from jax import lax

LAYER_COUNT = 128
NTR = 8
COLS_DEV = 4096
HALO = 1024
STRIP_VERTICALS = 131072


def draw_adjacency_table(key, part):
    magnitude = jax.random.randint(jax.random.fold_in(key, 11), (6, STRIP_VERTICALS), 1, HALO + 1)
    sign_choice = jax.random.randint(jax.random.fold_in(key, 12), (6, STRIP_VERTICALS), 0, 2) * 2 - 1
    offsets = magnitude * sign_choice
    position = jnp.arange(STRIP_VERTICALS, dtype=jnp.int32) % COLS_DEV
    offsets = offsets.at[0].set(jnp.where(position == COLS_DEV - 1, HALO, offsets[0]))
    offsets = offsets.at[1].set(jnp.where(position == 0, -HALO, offsets[1]))
    return (position[None, :] + HALO + offsets).astype(jnp.int32)


def level_of(rng, shape, cuts, smallest, top_value):
    def one(dim, blocks):
        heights = jax.random.uniform(jax.random.fold_in(jax.random.fold_in(rng, 6), dim), (blocks,), jnp.float32, smallest / len(cuts), top_value / len(cuts))
        return jnp.repeat(jnp.exp(heights), shape[dim] // blocks).reshape((-1,) + (1,) * (len(shape) - dim - 1))

    gain = one(*cuts[0])
    for cut in cuts[1:]:
        gain = gain * one(*cut)
    return gain


def normal_values(own_key, extent, width, limit, shards=(), held_as=jnp.bfloat16):
    level = level_of(own_key, extent, shards, -0.22, 0.18) if shards else 1.0
    array = jax.random.normal(own_key, extent, jnp.float32) * width * level
    return jnp.minimum(jnp.maximum(array, -limit), limit).astype(held_as)


def setup_inputs(seed: int = 0) -> dict:
    key_list = jax.random.split(jax.random.key(seed), 9)
    return {
        "thermal_state": jnp.clip(0.5 + 1.0 * jax.random.uniform(key_list[0], (LAYER_COUNT, STRIP_VERTICALS), jnp.float32) ** level_of(key_list[0], (LAYER_COUNT, STRIP_VERTICALS), ((0, 4), (1, 32)), -0.2, 0.2), 0.5, 1.5),
        "humidity_loading": jnp.clip(1.0 * jax.random.uniform(key_list[1], (LAYER_COUNT, STRIP_VERTICALS), jnp.float32) ** level_of(key_list[1], (LAYER_COUNT, STRIP_VERTICALS), ((0, 4), (1, 32)), -0.2, 0.2), 0.0, 1.0),
        "interface_mixing_strength": jnp.clip(jnp.exp(math.log(30.0) - 3.4011974 * jax.random.uniform(key_list[2], (LAYER_COUNT, STRIP_VERTICALS), jnp.float32) ** level_of(key_list[2], (LAYER_COUNT, STRIP_VERTICALS), ((0, 4), (1, 32)), -0.2, 0.2)), 1.0, 30.0),
        "passive_species": normal_values(key_list[3], (NTR, LAYER_COUNT, STRIP_VERTICALS), 1.0, 6.0, ((1, 4), (2, 32))),
        "terrain_height": normal_values(key_list[4], (STRIP_VERTICALS,), 1.0, 6.0, ((0, 32),), jnp.float32),
        "log_bottom_stress": normal_values(key_list[5], (STRIP_VERTICALS,), 0.5, 3.0, ((0, 32),), jnp.float32),
        "side_length_share": jnp.clip(jnp.exp(math.log(2.0) - 1.3862944 * jax.random.uniform(key_list[6], (6, STRIP_VERTICALS), jnp.float32) ** level_of(key_list[6], (6, STRIP_VERTICALS), ((1, 32),), -0.2, 0.2)), 0.5, 2.0),
        "adjacency_table": draw_adjacency_table(jax.random.fold_in(key_list[8], 71), 0),
    }


humidity_multiplier = 0.608
mixing_rate = 0.05


def thomas_solve(sub_diagonal, diagonal, super_diagonal, right_side):
    def forward(carry, inputs):
        prev_ratio, prev_value = carry
        sub_row, diag_row, super_row, right_row = inputs
        divisor = diag_row - sub_row * prev_ratio
        ratio = super_row / divisor
        value = (right_row - sub_row[None] * prev_value) / divisor[None]
        return (ratio, value), (ratio, value)

    start_carry = (jnp.zeros(diagonal.shape[1:], jnp.float32), jnp.zeros(right_side.shape[1:], jnp.float32))
    _, (ratios, values) = lax.scan(forward, start_carry, (sub_diagonal, diagonal, super_diagonal, right_side))

    def backward(following, inputs):
        ratio, value = inputs
        solved = value - ratio[None] * following
        return solved, solved

    _, solved = lax.scan(backward, jnp.zeros(right_side.shape[1:], jnp.float32), (ratios, values), reverse=True)
    return solved


def reference(thermal_state, humidity_loading, interface_mixing_strength, passive_species, terrain_height, log_bottom_stress, side_length_share, adjacency_table):
    density_thermal = thermal_state * (1.0 + humidity_multiplier * humidity_loading)
    trailing_part = jnp.cumsum(density_thermal[::-1], axis=0)[::-1]
    gravity_height = terrain_height[None, :] + (trailing_part - 0.5 * density_thermal) / LAYER_COUNT
    column_ids = jnp.arange(STRIP_VERTICALS, dtype=jnp.int32)
    tile_start = (column_ids // COLS_DEV) * COLS_DEV
    tracer_values = passive_species.astype(jnp.float32)
    force_divergence = jnp.zeros_like(gravity_height)
    laplace = jnp.zeros_like(tracer_values)
    for direction in range(6):
        target = ((tile_start + adjacency_table[direction] - HALO) % STRIP_VERTICALS).astype(jnp.int32)
        stencil_entries = side_length_share[direction][None, :]
        height_jump = gravity_height[:, target] - gravity_height
        stress_jump = log_bottom_stress[target] - log_bottom_stress
        force_divergence = force_divergence + stencil_entries * (height_jump + density_thermal * stress_jump[None, :])
        laplace = laplace + stencil_entries[None] * (tracer_values[:, :, target] - tracer_values)
    mixed = tracer_values + mixing_rate * laplace
    layer_indices = jnp.arange(LAYER_COUNT, dtype=jnp.int32)
    gas_constant_share = jnp.where(layer_indices[:, None] == 0, 0.0, interface_mixing_strength * density_thermal)
    below_kappa = jnp.concatenate([gas_constant_share[1:], jnp.zeros((1, STRIP_VERTICALS), jnp.float32)], axis=0)
    diagonal = 1.0 + gas_constant_share + below_kappa
    solved = thomas_solve(-gas_constant_share, diagonal, -below_kappa, jnp.moveaxis(mixed, 1, 0))
    new_tracers = jnp.moveaxis(solved, 0, 1)
    return (gravity_height, force_divergence, new_tracers)
```

```python
import jax
import jax.numpy as jnp
from jax import lax
from jax.experimental import pallas as pl
from jax.experimental.pallas import tpu as pltpu
from jax.sharding import PartitionSpec as P

BF = jnp.bfloat16
F32 = jnp.float32
MESH = pl.DeviceIdType.MESH
HALO = 1024
COLS = 4096
EXT = COLS + 2 * HALO
LEV = 32
NTR = 8
BLK = 256
WIN = BLK + 2 * HALO
NBLK = COLS // BLK
GRP = 512
ROWS = 336
TILES = 32
LEVELS = 128.0

R_SUM = 0
R_KAP = 3
R_TRC = 4
R_VIR = 20
R_BAS = 22
R_COF = 24
R_CHP = 25
R_YB = 26
R_YC = 29
N_REMOTE = 32

L_NAT = 0
L_FOLD = 2
L_TRC = 26
L_SMALL = 34
N_LOCAL = 38
L_OUT = 38
N_OUT = 51
SPANS = ((1024, 2048), (0, 1024), (3072, 1024))


def kernel(
    th_ref, hu_ref, mx_ref, tr_ref, te_ref, lo_ref, sh_ref, ad_ref,
    y_out, ends_out, g_out, h_out, gh_out, fo_out,
    xa, w, mm, fo, gh, vn, tn, hn, tf, hf, sf,
    rf, pf, ef, gf, hfo, sums, kbot, ktop, vb, vh, bl, blh,
    cfo, cfi, cho, chi, dq, yb, yp, yc, yo, xe, ter, los, shr, adj, shm, shi, slo, tot,
    ssem, rsem, lsem,
):
    tile = lax.axis_index("tile")
    lev = lax.axis_index("lev")
    core = lev % 2
    chip = lev // 2
    partner = chip * 2 + 1 - core
    across = (lev + 2) % 4
    diagonal = (partner + 2) % 4
    above = (lev + 3) % 4
    nxt = ((tile + 1) % TILES, lev)
    prv = ((tile + TILES - 1) % TILES, lev)
    peers = ((tile, partner), (tile, across), (tile, diagonal))

    bar = pltpu.get_barrier_semaphore()
    for q in peers + (nxt, prv):
        pl.semaphore_signal(bar, inc=1, device_id=q, device_id_type=MESH)

    def remote(i, src, dst, to):
        return pltpu.make_async_remote_copy(
            src_ref=src, dst_ref=dst, send_sem=ssem.at[i], recv_sem=rsem.at[i],
            device_id=to, device_id_type=MESH)

    nat = [pltpu.make_async_copy(s, d, lsem.at[L_NAT + i]) for i, (s, d) in enumerate(((th_ref, tn), (hu_ref, hn)))]
    small = [
        pltpu.make_async_copy(s, d, lsem.at[L_SMALL + i])
        for i, (s, d) in enumerate(((te_ref, ter), (lo_ref, los), (sh_ref, shr), (ad_ref, adj)))
    ]
    fold = []
    for i, (s, d) in enumerate(((th_ref, tf), (hu_ref, hf), (mx_ref, sf))):
        for g in range(8):
            fold.append(
                pltpu.make_async_copy(s.at[:, pl.ds(GRP * g, GRP)], d.at[:, g, :], lsem.at[L_FOLD + 8 * i + g])
            )
    trc = [
        pltpu.make_async_copy(tr_ref.at[n], xa.at[pl.ds(LEV * n, LEV), pl.ds(HALO, COLS)], lsem.at[L_TRC + n])
        for n in range(NTR)
    ]
    for c in nat + fold + small + trc:
        c.start()

    row = lax.broadcasted_iota(jnp.int32, (48, LEV), 0)
    col = lax.broadcasted_iota(jnp.int32, (48, LEV), 1)
    tri = jnp.where(row >= LEV, 1.0, jnp.where(col > row, 1.0, jnp.where(col == row, 0.5, 0.0))).astype(BF)
    for c in nat:
        c.wait()

    def natural(i, _):
        cs = pl.ds(pl.multiple_of(i * GRP, GRP), GRP)
        v = tn[:, cs] * (1.0 + 0.608 * hn[:, cs])
        vn[:, cs] = v
        v1 = v.astype(BF)
        vb[:, cs] = v1
        rest = v - v1.astype(F32)
        v2 = rest.astype(BF)
        v3 = (rest - v2.astype(F32)).astype(BF)
        part = jnp.dot(tri, v1, preferred_element_type=F32)
        part = part + jnp.dot(tri, v2, preferred_element_type=F32)
        part = part + jnp.dot(tri, v3, preferred_element_type=F32)
        gh[:, cs] = part[:LEV]
        sums[0, :, cs] = part[LEV : LEV + 1]
        return 0

    lax.fori_loop(0, 8, natural, 0)
    for c in fold:
        c.wait()
    for k in range(LEV):
        kap = sf[k] * (tf[k] * (1.0 + 0.608 * hf[k]))
        if k == 0:
            kap = jnp.where(lev == 0, 0.0, kap)
            ktop[...] = kap
        sf[k] = kap

    pl.semaphore_wait(bar, 5)
    c_sum = [remote(R_SUM + d, sums.at[0], sums.at[1 + d], peers[d]) for d in range(3)]
    c_kap = remote(R_KAP, ktop, kbot, (tile, above))
    for c in c_sum:
        c.start()
    c_kap.start()
    c_trc = []
    for n in range(NTR):
        rows = pl.ds(LEV * n, LEV)
        c_trc.append(remote(R_TRC + n, tr_ref.at[n, :, pl.ds(COLS - HALO, HALO)], xa.at[rows, pl.ds(0, HALO)], nxt))
        c_trc.append(
            remote(R_TRC + 8 + n, tr_ref.at[n, :, pl.ds(0, HALO)], xa.at[rows, pl.ds(HALO + COLS, HALO)], prv)
        )
    for c in c_trc:
        c.start()

    c_kap.wait_recv()
    e = None
    gg = None
    for k in range(LEV):
        a = sf[k]
        below = sf[k + 1] if k < LEV - 1 else kbot[...]
        d = 1.0 + a + below
        if k:
            d = d - a * e
        r = 1.0 / d
        p = a * r
        e = below * r
        gg = p * gg if k else p
        rf[k] = r
        pf[k] = p
        ef[k] = e
        gf[k] = gg
    hh = e
    hfo[LEV - 1] = hh
    cfo[1] = gg
    cfo[3] = hh
    for k in range(LEV - 2, -1, -1):
        e = ef[k]
        gg = gf[k] + e * gg
        hh = e * hh
        gf[k] = gg
        hfo[k] = hh
    cfo[0] = gg
    cfo[2] = hh
    c_cof = remote(R_COF, cfo, cfi, (tile, partner))
    c_cof.start()

    for c in small:
        c.wait()
    for c in c_sum:
        c.wait_recv()
    peer_levs = (partner, across, diagonal)

    def split(v):
        hi = v.astype(BF)
        return hi, (v - hi.astype(F32)).astype(BF)

    sub16 = lax.broadcasted_iota(jnp.int32, (16, GRP), 0)

    def put_extra(cs, height, stress):
        hi, low = split(height)
        xa[pl.ds(256, LEV), cs] = hi
        xa[pl.ds(304, LEV), cs] = low
        shi_, slo_ = split(stress)
        both = jnp.where(
            sub16 == 0,
            jnp.broadcast_to(shi_.astype(F32), (16, GRP)),
            jnp.where(sub16 == 1, jnp.broadcast_to(slo_.astype(F32), (16, GRP)), 0.0),
        )
        xa[pl.ds(288, 16), cs] = both.astype(BF)

    def heights(i, _):
        cs = pl.ds(pl.multiple_of(i * GRP, GRP), GRP)
        below = jnp.zeros((1, GRP), F32)
        for d in range(3):
            below = below + jnp.where(peer_levs[d] > lev, sums[1 + d, :, cs], 0.0)
        base = ter[:, cs] + below / LEVELS
        stress = los[:, cs]
        bl[pl.ds(0, 1), cs] = base
        bl[pl.ds(1, 1), cs] = stress
        height = base + gh[:, cs] / LEVELS
        gh[:, cs] = height
        put_extra(pl.ds(pl.multiple_of(HALO + i * GRP, GRP), GRP), height, stress)
        return 0

    lax.fori_loop(0, 8, heights, 0)
    c_hal = []
    for d, (lo, to) in enumerate(((COLS - HALO, nxt), (0, prv))):
        c_hal.append(remote(R_VIR + d, vb.at[:, pl.ds(lo, HALO)], vh.at[d], to))
        c_hal.append(remote(R_BAS + d, bl.at[:, pl.ds(lo, HALO)], blh.at[d], to))
    for c in c_hal:
        c.start()
    out_gh = pltpu.make_async_copy(gh, gh_out, lsem.at[L_OUT])
    out_gh.start()

    t = [adj[pl.ds(m, 1), :] for m in range(6)]
    s = [shr[pl.ds(m, 1), :] for m in range(6)]
    total = s[0]
    for m in range(1, 6):
        total = total + s[m]
    tot[...] = total
    for m in range(6):
        acc = s[m]
        for q in range(m):
            acc = acc + jnp.where(t[q] == t[m], s[q], 0.0)
        shm[pl.ds(m, 1), :] = acc
    merged = shm[...]
    high = merged.astype(BF)
    shi[...] = high
    slo[...] = (merged - high.astype(F32)).astype(BF)

    def weights(j, _):
        cs = pl.ds(pl.multiple_of(j * BLK, BLK), BLK)
        place = (adj[:, cs] - j * BLK).astype(F32)
        high = shi[:, cs]
        low = slo[:, cs]
        ids = lax.broadcasted_iota(jnp.int32, (BLK, BLK), 0).astype(F32).astype(BF)
        hs = [jnp.broadcast_to(high[m : m + 1], (BLK, BLK)) for m in range(6)]
        ls = [jnp.broadcast_to(low[m : m + 1], (BLK, BLK)) for m in range(6)]
        for r in range(9):
            u = jnp.clip(place - float(BLK * r), -1.0, float(BLK)).astype(BF)
            wh = jnp.zeros((BLK, BLK), BF)
            wl = jnp.zeros((BLK, BLK), BF)
            for m in range(6):
                hit = jnp.broadcast_to(u[m : m + 1], (BLK, BLK)) == ids
                wh = jnp.where(hit, hs[m], wh)
                wl = jnp.where(hit, ls[m], wl)
            w[j, 0, pl.ds(BLK * r, BLK), :] = wh
            w[j, 1, pl.ds(BLK * r, BLK), :] = wl
        return 0

    def product(j, lo, hi, rows, wide):
        n = BLK * (hi - lo)
        x = xa[rows, pl.ds(pl.multiple_of(BLK * (j + lo), BLK), n)]
        ws = pl.ds(BLK * lo, n)
        return jnp.dot(x, w[j, 0, ws, :], preferred_element_type=F32) + jnp.dot(
            x, w[j, 1, ws, :], preferred_element_type=F32
        )

    def own_part(j, lo, hi):
        cs = pl.ds(pl.multiple_of(j * BLK, BLK), BLK)
        es = pl.ds(pl.multiple_of(HALO + j * BLK, BLK), BLK)
        a = product(j, lo, hi, pl.ds(0, ROWS), True)
        total = tot[:, cs]
        own = xa[pl.ds(0, 256), es].astype(F32)
        mixed = own * (1.0 - 0.05 * total) + 0.05 * a[:256]
        mm[2 * j] = mixed[:, :128]
        mm[2 * j + 1] = mixed[:, 128:]
        stress = a[288:289] + a[289:290] - los[:, cs] * total
        fo[:, cs] = (a[256:288] + a[304:336] - gh[:, cs] * total) + vn[:, cs] * stress

    for c in trc:
        c.wait()
    lax.fori_loop(0, NBLK, weights, 0)

    def interior(i, _):
        own_part(4 + i, 0, 9)
        return 0

    lax.fori_loop(0, 8, interior, 0)

    def bc(ref, k, g):
        return jnp.broadcast_to(ref[k, pl.ds(g, 1), :], (NTR, GRP))

    def solve(g):
        def lane(ref, k, q):
            return jnp.broadcast_to(ref[k, pl.ds(g, 1), pl.ds(128 * q, 128)], (NTR, 128))

        def at(k):
            return pl.ds(k, NTR, stride=LEV)

        f = [None] * 4
        for k in range(LEV):
            for q in range(4):
                v = mm[4 * g + q, at(k), :] * lane(rf, k, q)
                f[q] = v + lane(pf, k, q) * f[q] if k else v
                mm[4 * g + q, at(k), :] = f[q]
        for q in range(4):
            yb[1, :, pl.ds(g * GRP + 128 * q, 128)] = f[q]
        for k in range(LEV - 2, -1, -1):
            for q in range(4):
                f[q] = mm[4 * g + q, at(k), :] + lane(ef, k, q) * f[q]
                mm[4 * g + q, at(k), :] = f[q]
        for q in range(4):
            yb[0, :, pl.ds(g * GRP + 128 * q, 128)] = f[q]

    def ends(i):
        cs = pl.ds(*SPANS[i])
        return remote(R_YB + i, yb.at[:, :, cs], yp.at[:, :, cs], (tile, partner))

    def chips(i):
        cs = pl.ds(*SPANS[i])
        return remote(R_YC + i, yc.at[:, cs], yo.at[:, cs], (tile, across))

    c_yb = [ends(i) for i in range(3)]
    c_yc = [chips(i) for i in range(3)]

    for g in range(2, 6):
        solve(g)
    c_yb[0].start()

    c_cof.wait_recv()
    upper = core == 0

    def pick(i, j):
        return jnp.where(upper, cfo[i], cfi[i]), jnp.where(upper, cfi[j], cfo[j])

    g_bu, g_bl = pick(1, 1)
    g_tu, g_tl = pick(0, 0)
    h_tu, h_tl = pick(2, 2)
    h_bu, h_bl = pick(3, 3)
    dd = 1.0 / (1.0 - g_tl * h_bu)
    mine = jnp.where(chip == 0, h_bl + g_bl * h_bu * dd * h_tl, g_tu + h_tu * dd * g_tl * g_bu)
    cho[...] = mine
    dq[0] = dd
    dq[1] = dd * (g_tl * g_bu + h_tl)
    dq[2] = g_tl
    dq[3] = h_bu
    dq[4] = g_bu
    dq[5] = g_bl
    dq[6] = h_tu
    c_chp = remote(R_CHP, cho, chi, (tile, across))
    c_chp.start()

    def merge(g):
        cs = pl.ds(g * GRP, GRP)
        yt_u = jnp.where(upper, yb[0, :, cs], yp[0, :, cs])
        yb_u = jnp.where(upper, yb[1, :, cs], yp[1, :, cs])
        yt_l = jnp.where(upper, yp[0, :, cs], yb[0, :, cs])
        yb_l = jnp.where(upper, yp[1, :, cs], yb[1, :, cs])
        t0 = bc(dq, 0, g) * (yt_l + bc(dq, 2, g) * yb_u)
        y0 = yb_l + bc(dq, 5, g) * (yb_u + bc(dq, 3, g) * t0)
        y1 = yt_u + bc(dq, 6, g) * t0
        yc[:, cs] = jnp.where(chip == 0, y0, y1)
        xe[0, :, cs] = t0
        xe[1, :, cs] = yb_u

    def finish(g):
        cs = pl.ds(g * GRP, GRP)
        one = pl.ds(g, 1)
        cm = cho[one, :]
        co = chi[one, :]
        scale = jnp.broadcast_to(1.0 / (1.0 - cm * co), (NTR, GRP))
        other = scale * (yo[:, cs] + jnp.broadcast_to(co, (NTR, GRP)) * yc[:, cs])
        t_l = xe[0, :, cs] + bc(dq, 1, g) * other
        b_u = xe[1, :, cs] + bc(dq, 3, g) * t_l + bc(dq, 4, g) * other
        xe[0, :, cs] = jnp.where(upper, other, b_u)
        xe[1, :, cs] = jnp.where(upper, t_l, other)

    out_g = []
    for g in range(8):
        hs = pl.ds(GRP * g, GRP)
        out_g.append(pltpu.make_async_copy(gf.at[:, g, :], g_out.at[:, hs], lsem.at[L_OUT + 1 + g]))
        out_g.append(pltpu.make_async_copy(hfo.at[:, g, :], h_out.at[:, hs], lsem.at[L_OUT + 9 + g]))
    for c in out_g:
        c.start()

    for j in range(4):
        own_part(j, 4 - j, 9)
        own_part(15 - j, 0, 5 + j)

    c_yb[0].wait_recv()

    for g in range(2, 6):
        merge(g)
    c_yc[0].start()

    for c in c_trc:
        c.wait_recv()
    for j in range(4):
        for b, lo, hi in ((j, 0, 4 - j), (15 - j, 5 + j, 9)):
            a = product(b, lo, hi, pl.ds(0, 256), False)
            mm[2 * b] = mm[2 * b] + 0.05 * a[:, :128]
            mm[2 * b + 1] = mm[2 * b + 1] + 0.05 * a[:, 128:]

    edges = (0, 1, 6, 7)
    for g in edges:
        solve(g)
    c_yb[1].start()
    c_yb[2].start()
    out_y = [
        pltpu.make_async_copy(mm.at[b], y_out.at[:, pl.ds(128 * b, 128)], lsem.at[L_OUT + 19 + b]) for b in range(32)
    ]
    for c in out_y:
        c.start()
    c_yb[1].wait_recv()
    c_yb[2].wait_recv()

    for g in edges:
        merge(g)
    c_yc[1].start()
    c_yc[2].start()

    for c in c_hal:
        c.wait_recv()
    for d in range(2):
        for i in range(2):
            cs = pl.ds(GRP * i, GRP)
            part = jnp.dot(tri[:LEV], vh[d, :, cs], preferred_element_type=F32)
            put_extra(
                pl.ds(d * (HALO + COLS) + GRP * i, GRP),
                blh[d, pl.ds(0, 1), cs] + part / LEVELS,
                blh[d, pl.ds(1, 1), cs],
            )
    for j in range(4):
        for b, lo, hi in ((j, 0, 4 - j), (15 - j, 5 + j, 9)):
            a = product(b, lo, hi, pl.ds(256, 80), False)
            cs = pl.ds(b * BLK, BLK)
            fo[:, cs] = fo[:, cs] + (a[:32] + a[48:80]) + vn[:, cs] * (a[32:33] + a[33:34])
    out_fo = pltpu.make_async_copy(fo, fo_out, lsem.at[L_OUT + 17])
    out_fo.start()

    c_chp.wait_recv()
    for c in c_yc:
        c.wait_recv()

    for g in range(8):
        finish(g)
    out_e = pltpu.make_async_copy(xe, ends_out, lsem.at[L_OUT + 18])
    out_e.start()

    for c in c_sum + [c_kap, c_cof, c_chp] + c_trc + c_hal + c_yb + c_yc:
        c.wait_send()
    for c in [out_gh] + out_g + out_y + [out_fo, out_e]:
        c.wait()


def combine(y_ref, e_ref, g_ref, h_ref, gh_ref, fo_ref, gh_out, fo_out, x_out):
    g = g_ref[...]
    h = h_ref[...]
    for n in range(NTR):
        x_out[n] = y_ref[n] + g * e_ref[0, pl.ds(n, 1), :] + h * e_ref[1, pl.ds(n, 1), :]
    gh_out[...] = gh_ref[...]
    fo_out[...] = fo_ref[...]


def local(thermal, humid, mixing, tracers, terrain, stress, share, table):
    f32 = lambda *s: jax.ShapeDtypeStruct(s, F32)
    vm = lambda *s: pltpu.VMEM(s, F32)
    vb = lambda *s: pltpu.VMEM(s, BF)
    fold = vm(LEV, 8, GRP)
    nat = vm(LEV, COLS)
    anyspec = pl.BlockSpec(memory_space=pl.ANY)
    y, ends, g, h, gh, fo = pl.pallas_call(
        kernel,
        out_shape=(f32(NTR * LEV, COLS), f32(2, NTR, COLS), f32(LEV, COLS), f32(LEV, COLS), f32(LEV, COLS), f32(LEV, COLS)),
        in_specs=[anyspec] * 8,
        out_specs=(anyspec,) * 6,
        scratch_shapes=[
            vb(ROWS, EXT), vb(NBLK, 2, WIN, BLK), vm(32, 256, 128), nat, nat, nat, nat, nat, fold, fold, fold,
            fold, fold, fold, fold, fold, vm(4, 1, COLS), vm(8, GRP), vm(8, GRP),
            vb(LEV, COLS), vb(2, LEV, HALO), vm(2, COLS), vm(2, 2, HALO),
            vm(4, 8, GRP), vm(4, 8, GRP), vm(8, GRP), vm(8, GRP), vm(7, 8, GRP),
            vm(2, NTR, COLS), vm(2, NTR, COLS), vm(NTR, COLS), vm(NTR, COLS), vm(2, NTR, COLS),
            vm(1, COLS), vm(1, COLS), vm(6, COLS), pltpu.VMEM((6, COLS), jnp.int32),
            vm(6, COLS), vb(6, COLS), vb(6, COLS), vm(1, COLS),
            pltpu.SemaphoreType.DMA((N_REMOTE,)), pltpu.SemaphoreType.DMA((N_REMOTE,)),
            pltpu.SemaphoreType.DMA((N_LOCAL + N_OUT,)),
        ],
        compiler_params=pltpu.CompilerParams(collective_id=0, has_side_effects=True, vmem_limit_bytes=67000000),
        name="band",
    )(thermal, humid, mixing, tracers, terrain[None], stress[None], share, table)
    width = 1024
    full = lambda *lead: pl.BlockSpec(lead + (width,), lambda i: (0,) * len(lead) + (i,))
    gh2, fo2, x = pl.pallas_call(
        combine,
        grid=(COLS // width,),
        out_shape=(f32(LEV, COLS), f32(LEV, COLS), f32(NTR, LEV, COLS)),
        in_specs=[full(NTR, LEV), full(2, NTR), full(LEV), full(LEV), full(LEV), full(LEV)],
        out_specs=(full(LEV), full(LEV), full(NTR, LEV)),
        name="combine",
    )(y.reshape(NTR, LEV, COLS), ends, g, h, gh, fo)
    return gh2, fo2, x


def solution(mesh):
    return jax.shard_map(
        local,
        mesh=mesh,
        in_specs=(
            P("lev", "tile"), P("lev", "tile"), P("lev", "tile"), P(None, "lev", "tile"),
            P("tile"), P("tile"), P(None, "tile"), P(None, "tile"),
        ),
        out_specs=(P("lev", "tile"), P("lev", "tile"), P(None, "lev", "tile")),
        check_vma=False,
    )
```

```python
import jax
import jax.numpy as jnp
from jax import lax
from jax.experimental import pallas as pl
from jax.experimental.pallas import tpu as pltpu
from jax.sharding import PartitionSpec as P

BF = jnp.bfloat16
F32 = jnp.float32
MESH = pl.DeviceIdType.MESH
HALO = 1024
COLS = 4096
EXT = COLS + 2 * HALO
LEV = 32
NTR = 8
BLK = 256
WIN = BLK + 2 * HALO
NBLK = COLS // BLK
GRP = 512
ROWS = 336
TILES = 32
LEVELS = 128.0

R_SUM = 0
R_KAP = 3
R_TRC = 4
R_VIR = 12
R_BAS = 14
R_COF = 16
R_CHP = 17
R_YB = 18
R_YC = 23
N_REMOTE = 28

L_NAT = 0
L_FOLD = 2
L_TRC = 26
L_SMALL = 34
N_LOCAL = 38
L_OUT = 38
N_OUT = 24
PART = 3
SPANS = ((1024, 2048), (512, 512), (3072, 512), (0, 512), (3584, 512))


def kernel(
    th_ref, hu_ref, mx_ref, tr_ref, te_ref, lo_ref, sh_ref, ad_ref,
    y_out, ends_out, g_out, h_out, gh_out, fo_out,
    xa, xh, xg, w0, w1, wh, mm, yk, fo, gh, vn, tn, hn, tf, hf, sf,
    rf, pf, ef, gf, hfo, sums, kbot, ktop, vb, vh, bl, blh,
    cfo, cfi, cho, chi, dq, yb, yp, yc, yo, xe, ter, los, shr, adj, shm, shi, slo, tot,
    ssem, rsem, lsem,
):
    tile = lax.axis_index("tile")
    lev = lax.axis_index("lev")
    core = lev % 2
    chip = lev // 2
    partner = chip * 2 + 1 - core
    across = (lev + 2) % 4
    diagonal = (partner + 2) % 4
    above = (lev + 3) % 4
    nxt = ((tile + 1) % TILES, lev)
    prv = ((tile + TILES - 1) % TILES, lev)
    peers = ((tile, partner), (tile, across), (tile, diagonal))

    bar = pltpu.get_barrier_semaphore()
    for q in peers + (nxt, prv):
        pl.semaphore_signal(bar, inc=1, device_id=q, device_id_type=MESH)

    def remote(i, src, dst, to):
        return pltpu.make_async_remote_copy(
            src_ref=src, dst_ref=dst, send_sem=ssem.at[i], recv_sem=rsem.at[i],
            device_id=to, device_id_type=MESH)

    nat = [pltpu.make_async_copy(s, d, lsem.at[L_NAT + i]) for i, (s, d) in enumerate(((th_ref, tn), (hu_ref, hn)))]
    small = [
        pltpu.make_async_copy(s, d, lsem.at[L_SMALL + i])
        for i, (s, d) in enumerate(((te_ref, ter), (lo_ref, los), (sh_ref, shr), (ad_ref, adj)))
    ]
    fold = []
    for i, (s, d) in enumerate(((th_ref, tf), (hu_ref, hf), (mx_ref, sf))):
        for g in range(8):
            fold.append(
                pltpu.make_async_copy(s.at[:, pl.ds(GRP * g, GRP)], d.at[:, g, :], lsem.at[L_FOLD + 8 * i + g])
            )
    trc = [
        pltpu.make_async_copy(tr_ref.at[n], xa.at[pl.ds(LEV * n, LEV), pl.ds(HALO, COLS)], lsem.at[L_TRC + n])
        for n in range(NTR)
    ]
    for c in nat + fold + small + trc:
        c.start()
    xa[:, pl.ds(0, HALO)] = jnp.zeros((ROWS, HALO), BF)
    xa[:, pl.ds(HALO + COLS, HALO)] = jnp.zeros((ROWS, HALO), BF)

    row = lax.broadcasted_iota(jnp.int32, (48, LEV), 0)
    col = lax.broadcasted_iota(jnp.int32, (48, LEV), 1)
    tri = jnp.where(row >= LEV, 1.0, jnp.where(col > row, 1.0, jnp.where(col == row, 0.5, 0.0))).astype(BF)
    for c in nat:
        c.wait()

    def natural(i, _):
        cs = pl.ds(pl.multiple_of(i * GRP, GRP), GRP)
        v = tn[:, cs] * (1.0 + 0.608 * hn[:, cs])
        vn[:, cs] = v
        v1 = v.astype(BF)
        vb[:, cs] = v1
        rest = v - v1.astype(F32)
        v2 = rest.astype(BF)
        v3 = (rest - v2.astype(F32)).astype(BF)
        part = jnp.dot(tri, v1, preferred_element_type=F32)
        part = part + jnp.dot(tri, v2, preferred_element_type=F32)
        part = part + jnp.dot(tri, v3, preferred_element_type=F32)
        gh[:, cs] = part[:LEV]
        sums[0, :, cs] = part[LEV : LEV + 1]
        return 0

    lax.fori_loop(0, 8, natural, 0)
    for c in fold:
        c.wait()
    for k in range(LEV):
        kap = sf[k] * (tf[k] * (1.0 + 0.608 * hf[k]))
        if k == 0:
            kap = jnp.where(lev == 0, 0.0, kap)
            ktop[...] = kap
        sf[k] = kap

    def step(k, below, e, gg):
        a = sf[k]
        d = 1.0 + a + below
        if k:
            d = d - a * e
        r = 1.0 / d
        p = a * r
        e = below * r
        gg = p * gg if k else p
        rf[k] = r
        pf[k] = p
        ef[k] = e
        gf[k] = gg
        return r, p, e, gg

    e = None
    gg = None
    for k in range(LEV - 1):
        _, _, e, gg = step(k, sf[k + 1], e, gg)
    for c in small:
        c.wait()

    t = [adj[pl.ds(m, 1), :] for m in range(6)]
    s = [shr[pl.ds(m, 1), :] for m in range(6)]
    total = s[0]
    for m in range(1, 6):
        total = total + s[m]
    tot[...] = total
    for m in range(6):
        acc = s[m]
        for q in range(m):
            acc = acc + jnp.where(t[q] == t[m], s[q], 0.0)
        shm[pl.ds(m, 1), :] = acc
    merged = shm[...]
    high = merged.astype(BF)
    shi[...] = high
    slo[...] = (merged - high.astype(F32)).astype(BF)

    ids = lax.broadcasted_iota(jnp.int32, (BLK, BLK), 0).astype(F32).astype(BF)

    def tables(j):
        cs = pl.ds(pl.multiple_of(j * BLK, BLK), BLK)
        place = (adj[:, cs] - j * BLK).astype(F32)
        high = shi[:, cs]
        low = slo[:, cs]
        hs = [jnp.broadcast_to(high[m : m + 1], (BLK, BLK)) for m in range(6)]
        ls = [jnp.broadcast_to(low[m : m + 1], (BLK, BLK)) for m in range(6)]
        return place, hs, ls

    def chunk(tab, offset):
        place, hs, ls = tab
        u = jnp.clip(place - offset, -1.0, float(BLK)).astype(BF)
        hi = jnp.zeros((BLK, BLK), BF)
        lw = jnp.zeros((BLK, BLK), BF)
        for m in range(6):
            hit = jnp.broadcast_to(u[m : m + 1], (BLK, BLK)) == ids
            hi = jnp.where(hit, hs[m], hi)
            lw = jnp.where(hit, ls[m], lw)
        return hi, lw

    def build(tab, w, r):
        hi, lw = chunk(tab, float(BLK * r))
        w[0, pl.ds(BLK * r, BLK), :] = hi
        w[1, pl.ds(BLK * r, BLK), :] = lw

    first = tables(4)
    for r in range(9):
        build(first, w0, r)

    pl.semaphore_wait(bar, 5)
    c_sum = [remote(R_SUM + d, sums.at[0], sums.at[1 + d], peers[d]) for d in range(3)]
    c_kap = remote(R_KAP, ktop, kbot, (tile, above))
    for c in c_sum:
        c.start()
    c_kap.start()
    c_trc = {}
    for i in range(4):
        for d, q, to in ((0, 3 - i, nxt), (1, i, prv)):
            src = tr_ref.at[:, :, pl.ds((COLS - HALO if d == 0 else 0) + BLK * q, BLK)]
            c_trc[d, q] = remote(R_TRC + 4 * d + q, src, xh.at[d, :, :, pl.ds(BLK * q, BLK)], to)
            c_trc[d, q].start()

    c_kap.wait_recv()
    r, p, e, gg = step(LEV - 1, kbot[...], e, gg)
    hh = e
    hfo[LEV - 1] = hh
    cfo[1] = gg
    cfo[3] = hh
    for k in range(LEV - 2, -1, -1):
        e = ef[k]
        gg = gf[k] + e * gg
        hh = e * hh
        gf[k] = gg
        hfo[k] = hh
    cfo[0] = gg
    cfo[2] = hh
    c_cof = remote(R_COF, cfo, cfi, (tile, partner))
    c_cof.start()

    for c in c_sum:
        c.wait_recv()
    peer_levs = (partner, across, diagonal)

    def split(v):
        hi = v.astype(BF)
        return hi, (v - hi.astype(F32)).astype(BF)

    sub16 = lax.broadcasted_iota(jnp.int32, (16, GRP), 0)

    def put_extra(ref, r0, cs, height, stress):
        hi, low = split(height)
        ref[pl.ds(r0, LEV), cs] = hi
        ref[pl.ds(r0 + 48, LEV), cs] = low
        shi_, slo_ = split(stress)
        both = jnp.where(
            sub16 == 0,
            jnp.broadcast_to(shi_.astype(F32), (16, GRP)),
            jnp.where(sub16 == 1, jnp.broadcast_to(slo_.astype(F32), (16, GRP)), 0.0),
        )
        ref[pl.ds(r0 + 32, 16), cs] = both.astype(BF)

    def heights(i, _):
        cs = pl.ds(pl.multiple_of(i * GRP, GRP), GRP)
        below = jnp.zeros((1, GRP), F32)
        for d in range(3):
            below = below + jnp.where(peer_levs[d] > lev, sums[1 + d, :, cs], 0.0)
        base = ter[:, cs] + below / LEVELS
        stress = los[:, cs]
        bl[pl.ds(0, 1), cs] = base
        bl[pl.ds(1, 1), cs] = stress
        height = base + gh[:, cs] / LEVELS
        gh[:, cs] = height
        put_extra(xa, 256, pl.ds(pl.multiple_of(HALO + i * GRP, GRP), GRP), height, stress)
        return 0

    lax.fori_loop(0, 8, heights, 0)
    c_hal = []
    for d, (lo, to) in enumerate(((COLS - HALO, nxt), (0, prv))):
        c_hal.append(remote(R_VIR + d, vb.at[:, pl.ds(lo, HALO)], vh.at[d], to))
        c_hal.append(remote(R_BAS + d, bl.at[:, pl.ds(lo, HALO)], blh.at[d], to))
    for c in c_hal:
        c.start()
    out_gh = pltpu.make_async_copy(gh, gh_out, lsem.at[L_OUT])
    out_gh.start()

    def fused(j, w, todo, lo=0, hi=9):
        parts = [range(q, min(q + PART, hi)) for q in range(lo, hi, PART)]
        share_out = -(-len(todo) // len(parts))
        high = None
        low = None
        for i, part in enumerate(parts):
            for work in todo[share_out * i : share_out * (i + 1)]:
                work()
            at = BLK * part[0]
            n = BLK * len(part)
            xs = pl.ds(pl.multiple_of(BLK * j, BLK) + at, n)
            d = jnp.dot(xa[:, xs], w[0, pl.ds(at, n), :], preferred_element_type=F32)
            high = d if high is None else high + d
            d = jnp.dot(xa[pl.ds(0, 304), xs], w[1, pl.ds(at, n), :], preferred_element_type=F32)
            low = d if low is None else low + d
        cs = pl.ds(pl.multiple_of(j * BLK, BLK), BLK)
        es = pl.ds(pl.multiple_of(HALO + j * BLK, BLK), BLK)
        total = tot[:, cs]
        own = xa[pl.ds(0, 256), es].astype(F32)
        mixed = own * (1.0 - 0.05 * total) + 0.05 * (high[:256] + low[:256])
        mm[2 * j] = mixed[:, :128]
        mm[2 * j + 1] = mixed[:, 128:]
        ends = high[288:290] + low[288:290]
        stress = ends[0:1] + ends[1:2] - los[:, cs] * total
        height = high[256:288] + low[256:288] + high[304:336]
        fo[:, cs] = (height - gh[:, cs] * total) + vn[:, cs] * stress

    def halo_product(c0, n, x):
        ws = pl.ds(BLK * c0, BLK * n)
        return jnp.dot(x, wh[0, ws, :], preferred_element_type=F32) + jnp.dot(
            x, wh[1, ws, :], preferred_element_type=F32
        )

    halo_parts = {}
    at = 0
    for j in range(4):
        halo_parts[j] = (at, 4 - j, 0, BLK * j)
        at += 4 - j
    for j in range(4):
        halo_parts[12 + j] = (at, j + 1, 1, 0)
        at += j + 1

    def own_range(b):
        return (4 - b, 9) if b < 4 else (0, 20 - b)

    def jobs(b, w, skip_own=False):
        tab = tables(b)
        lo, hi = own_range(b)
        c0 = halo_parts[b][0]

        def own(r):
            return lambda: build(tab, w, r)

        def far(i, r):
            def go():
                up, down = chunk(tab, float(BLK * r))
                ws = pl.ds(BLK * (c0 + i), BLK)
                wh[0, ws, :] = up
                wh[1, ws, :] = down

            return go

        beyond = [r for r in range(9) if not lo <= r < hi]
        out = [far(i, r) for i, r in enumerate(beyond)]
        return out if skip_own else [own(r) for r in range(lo, hi)] + out

    for c in trc:
        c.wait()

    def pair(i, _):
        j = 4 + 2 * i
        tab1 = tables(j + 1)
        fused(j, w0, [lambda r=r: build(tab1, w1, r) for r in range(9)])
        tab2 = tables(j + 2)
        fused(j + 1, w1, [lambda r=r: build(tab2, w0, r) for r in range(9)])
        return 0

    lax.fori_loop(0, 4, pair, 0)
    order = (12, 13, 14, 15, 3, 2, 1, 0)
    for i, b in enumerate(order):
        slot, other = (w0, w1) if i % 2 == 0 else (w1, w0)
        todo = jobs(order[i + 1], other) if i < 7 else []
        if i == 0:
            todo = todo + jobs(b, None, True)
        fused(b, slot, todo, *own_range(b))

    def bc(ref, k, g):
        return jnp.broadcast_to(ref[k, pl.ds(g, 1), :], (NTR, GRP))

    def solve(pair_of):
        chains = [(gi, q) for gi in pair_of for q in range(4)]

        def lane(ref, k, c):
            return jnp.broadcast_to(ref[k, pl.ds(c[0], 1), pl.ds(128 * c[1], 128)], (NTR, 128))

        f = [None] * 8
        for k in range(LEV):
            for i, c in enumerate(chains):
                b = 4 * c[0] + c[1]
                v = mm[b, pl.ds(k, NTR, stride=LEV), :] * lane(rf, k, c)
                f[i] = v + lane(pf, k, c) * f[i] if k else v
                yk[b, k] = f[i]
        for i, c in enumerate(chains):
            yb[1, :, pl.ds(c[0] * GRP + 128 * c[1], 128)] = f[i]
        for k in range(LEV - 2, -1, -1):
            for i, c in enumerate(chains):
                b = 4 * c[0] + c[1]
                f[i] = yk[b, k] + lane(ef, k, c) * f[i]
                yk[b, k] = f[i]
        for i, c in enumerate(chains):
            yb[0, :, pl.ds(c[0] * GRP + 128 * c[1], 128)] = f[i]

    def ends(i):
        cs = pl.ds(*SPANS[i])
        return remote(R_YB + i, yb.at[:, :, cs], yp.at[:, :, cs], (tile, partner))

    def chips(i):
        cs = pl.ds(*SPANS[i])
        return remote(R_YC + i, yc.at[:, cs], yo.at[:, cs], (tile, across))

    c_yb = [ends(i) for i in range(5)]
    c_yc = [chips(i) for i in range(5)]

    solve((2, 3))
    solve((4, 5))
    c_yb[0].start()
    runs = ((8, 16), (4, 4), (24, 4), (0, 4), (28, 4))

    def send_y(i):
        first, count = runs[i]

        def one(q, _):
            b = first + q
            ls = pl.ds(pl.multiple_of(b * 128, 128), 128)
            for n in range(NTR):
                pltpu.make_async_copy(yk.at[b, :, n, :], y_out.at[n, :, ls], lsem.at[L_OUT + 19 + i]).start()
            return 0

        lax.fori_loop(0, count, one, 0)

    def wait_y(i):
        first, count = runs[i]
        part = y_out.at[:, :, pl.ds(128 * first, 128 * count)]
        pltpu.make_async_copy(part, part, lsem.at[L_OUT + 19 + i]).wait()

    send_y(0)

    c_cof.wait_recv()
    upper = core == 0

    def pick(i, j):
        return jnp.where(upper, cfo[i], cfi[i]), jnp.where(upper, cfi[j], cfo[j])

    g_bu, g_bl = pick(1, 1)
    g_tu, g_tl = pick(0, 0)
    h_tu, h_tl = pick(2, 2)
    h_bu, h_bl = pick(3, 3)
    dd = 1.0 / (1.0 - g_tl * h_bu)
    mine = jnp.where(chip == 0, h_bl + g_bl * h_bu * dd * h_tl, g_tu + h_tu * dd * g_tl * g_bu)
    cho[...] = mine
    dq[0] = dd
    dq[1] = dd * (g_tl * g_bu + h_tl)
    dq[2] = g_tl
    dq[3] = h_bu
    dq[4] = g_bu
    dq[5] = g_bl
    dq[6] = h_tu
    c_chp = remote(R_CHP, cho, chi, (tile, across))
    c_chp.start()

    def merge(g):
        cs = pl.ds(g * GRP, GRP)
        yt_u = jnp.where(upper, yb[0, :, cs], yp[0, :, cs])
        yb_u = jnp.where(upper, yb[1, :, cs], yp[1, :, cs])
        yt_l = jnp.where(upper, yp[0, :, cs], yb[0, :, cs])
        yb_l = jnp.where(upper, yp[1, :, cs], yb[1, :, cs])
        t0 = bc(dq, 0, g) * (yt_l + bc(dq, 2, g) * yb_u)
        y0 = yb_l + bc(dq, 5, g) * (yb_u + bc(dq, 3, g) * t0)
        y1 = yt_u + bc(dq, 6, g) * t0
        yc[:, cs] = jnp.where(chip == 0, y0, y1)
        xe[0, :, cs] = t0
        xe[1, :, cs] = yb_u

    def finish(g):
        cs = pl.ds(g * GRP, GRP)
        one = pl.ds(g, 1)
        cm = cho[one, :]
        co = chi[one, :]
        scale = jnp.broadcast_to(1.0 / (1.0 - cm * co), (NTR, GRP))
        other = scale * (yo[:, cs] + jnp.broadcast_to(co, (NTR, GRP)) * yc[:, cs])
        t_l = xe[0, :, cs] + bc(dq, 1, g) * other
        b_u = xe[1, :, cs] + bc(dq, 3, g) * t_l + bc(dq, 4, g) * other
        xe[0, :, cs] = jnp.where(upper, other, b_u)
        xe[1, :, cs] = jnp.where(upper, t_l, other)

    out_g = []
    for g in range(8):
        hs = pl.ds(GRP * g, GRP)
        out_g.append(pltpu.make_async_copy(gf.at[:, g, :], g_out.at[:, hs], lsem.at[L_OUT + 1 + g]))
        out_g.append(pltpu.make_async_copy(hfo.at[:, g, :], h_out.at[:, hs], lsem.at[L_OUT + 9 + g]))
    for c in out_g:
        c.start()

    c_yb[0].wait_recv()

    for g in range(2, 6):
        merge(g)
    c_yc[0].start()

    stages = (
        (((0, 3), (1, 0), (0, 2), (1, 1)), (3, 12, 2, 13), (1, 6), (1, 2)),
        (((0, 1), (1, 2), (0, 0), (1, 3)), (1, 14, 0, 15), (0, 7), (3, 4)),
    )

    def join(groups, ids):
        for i in ids:
            c_yb[i].wait_recv()
        for g in groups:
            merge(g)
        for i in ids:
            c_yc[i].start()

    for chunks, blocks, groups, span_ids in stages:
        for key in chunks:
            c_trc[key].wait_recv()
        for b in blocks:
            c0, n, d, x0 = halo_parts[b]
            a = halo_product(c0, n, xh[d, :, :, pl.ds(x0, BLK * n)].reshape(256, BLK * n))
            mm[2 * b] = mm[2 * b] + 0.05 * a[:, :128]
            mm[2 * b + 1] = mm[2 * b + 1] + 0.05 * a[:, 128:]
        solve(groups)
        for i in span_ids:
            c_yb[i].start()
        for i in span_ids:
            send_y(i)
    join(*stages[0][2:])

    for c in c_hal:
        c.wait_recv()
    for d in range(2):
        for i in range(2):
            cs = pl.ds(GRP * i, GRP)
            part = jnp.dot(tri[:LEV], vh[d, :, cs], preferred_element_type=F32)
            put_extra(xg.at[d], 0, cs, blh[d, pl.ds(0, 1), cs] + part / LEVELS, blh[d, pl.ds(1, 1), cs])
    join(*stages[1][2:])
    for b, (c0, n, d, x0) in halo_parts.items():
        a = halo_product(c0, n, xg[d, :, pl.ds(x0, BLK * n)])
        cs = pl.ds(b * BLK, BLK)
        fo[:, cs] = fo[:, cs] + (a[:32] + a[48:80]) + vn[:, cs] * (a[32:33] + a[33:34])
    out_fo = pltpu.make_async_copy(fo, fo_out, lsem.at[L_OUT + 17])
    out_fo.start()

    c_chp.wait_recv()
    for c in c_yc:
        c.wait_recv()

    for g in range(8):
        finish(g)
    out_e = pltpu.make_async_copy(xe, ends_out, lsem.at[L_OUT + 18])
    out_e.start()

    for c in c_sum + [c_kap, c_cof, c_chp] + list(c_trc.values()) + c_hal + c_yb + c_yc:
        c.wait_send()
    for c in [out_gh] + out_g + [out_fo, out_e]:
        c.wait()
    for i in range(5):
        wait_y(i)


def combine(y_ref, e_ref, g_ref, h_ref, gh_ref, fo_ref, gh_out, fo_out, x_out):
    g = g_ref[...]
    h = h_ref[...]
    for n in range(NTR):
        x_out[n] = y_ref[n] + g * e_ref[0, pl.ds(n, 1), :] + h * e_ref[1, pl.ds(n, 1), :]
    gh_out[...] = gh_ref[...]
    fo_out[...] = fo_ref[...]


def local(thermal, humid, mixing, tracers, terrain, stress, share, table):
    f32 = lambda *s: jax.ShapeDtypeStruct(s, F32)
    vm = lambda *s: pltpu.VMEM(s, F32)
    vb = lambda *s: pltpu.VMEM(s, BF)
    fold = vm(LEV, 8, GRP)
    nat = vm(LEV, COLS)
    anyspec = pl.BlockSpec(memory_space=pl.ANY)
    y, ends, g, h, gh, fo = pl.pallas_call(
        kernel,
        out_shape=(f32(NTR, LEV, COLS), f32(2, NTR, COLS), f32(LEV, COLS), f32(LEV, COLS), f32(LEV, COLS), f32(LEV, COLS)),
        in_specs=[anyspec] * 8,
        out_specs=(anyspec,) * 6,
        scratch_shapes=[
            vb(ROWS, EXT), vb(2, NTR, LEV, HALO), vb(2, 80, HALO), vb(2, WIN, BLK), vb(2, WIN, BLK), vb(2, 20 * BLK, BLK),
            vm(32, 256, 128), vm(32, LEV, NTR, 128), nat, nat, nat, nat, nat, fold, fold, fold,
            fold, fold, fold, fold, fold, vm(4, 1, COLS), vm(8, GRP), vm(8, GRP),
            vb(LEV, COLS), vb(2, LEV, HALO), vm(2, COLS), vm(2, 2, HALO),
            vm(4, 8, GRP), vm(4, 8, GRP), vm(8, GRP), vm(8, GRP), vm(7, 8, GRP),
            vm(2, NTR, COLS), vm(2, NTR, COLS), vm(NTR, COLS), vm(NTR, COLS), vm(2, NTR, COLS),
            vm(1, COLS), vm(1, COLS), vm(6, COLS), pltpu.VMEM((6, COLS), jnp.int32),
            vm(6, COLS), vb(6, COLS), vb(6, COLS), vm(1, COLS),
            pltpu.SemaphoreType.DMA((N_REMOTE,)), pltpu.SemaphoreType.DMA((N_REMOTE,)),
            pltpu.SemaphoreType.DMA((N_LOCAL + N_OUT,)),
        ],
        compiler_params=pltpu.CompilerParams(collective_id=0, has_side_effects=True, vmem_limit_bytes=67000000),
        name="band",
    )(thermal, humid, mixing, tracers, terrain[None], stress[None], share, table)
    width = 1024
    full = lambda *lead: pl.BlockSpec(lead + (width,), lambda i: (0,) * len(lead) + (i,))
    gh2, fo2, x = pl.pallas_call(
        combine,
        grid=(COLS // width,),
        out_shape=(f32(LEV, COLS), f32(LEV, COLS), f32(NTR, LEV, COLS)),
        in_specs=[full(NTR, LEV), full(2, NTR), full(LEV), full(LEV), full(LEV), full(LEV)],
        out_specs=(full(LEV), full(LEV), full(NTR, LEV)),
        name="combine",
    )(y, ends, g, h, gh, fo)
    return gh2, fo2, x


def solution(mesh):
    return jax.shard_map(
        local,
        mesh=mesh,
        in_specs=(
            P("lev", "tile"), P("lev", "tile"), P("lev", "tile"), P(None, "lev", "tile"),
            P("tile"), P("tile"), P(None, "tile"), P(None, "tile"),
        ),
        out_specs=(P("lev", "tile"), P("lev", "tile"), P(None, "lev", "tile")),
        check_vma=False,
    )
```

```python
import jax
import jax.numpy as jnp
from jax import lax
from jax.experimental import pallas as pl
from jax.experimental.pallas import tpu as pltpu
from jax.sharding import PartitionSpec as P

BF = jnp.bfloat16
F32 = jnp.float32
MESH = pl.DeviceIdType.MESH
HALO = 1024
COLS = 4096
EXT = COLS + 2 * HALO
LEV = 32
NTR = 8
BLK = 256
WIN = BLK + 2 * HALO
NBLK = COLS // BLK
GRP = 512
ROWS = 336
TILES = 32
LEVELS = 128.0

R_SUM = 0
R_KAP = 3
R_TRC = 4
R_VIR = 12
R_BAS = 14
R_COF = 16
R_CHP = 17
R_YB = 18
R_YC = 23
N_REMOTE = 28

L_NAT = 0
L_FOLD = 2
L_TRC = 26
L_SMALL = 34
N_LOCAL = 38
L_OUT = 38
N_OUT = 24
PART = 1
SPANS = ((1024, 2048), (512, 512), (3072, 512), (0, 512), (3584, 512))


def kernel(
    th_ref, hu_ref, mx_ref, tr_ref, te_ref, lo_ref, sh_ref, ad_ref,
    y_out, ends_out, g_out, h_out, gh_out, fo_out,
    xa, xh, xg, w0, w1, wh, mm, yk, fo, gh, vn, tn, hn, tf, hf, sf,
    rf, pf, ef, gf, hfo, sums, kbot, ktop, vb, vh, bl, blh,
    cfo, cfi, cho, chi, dq, yb, yp, yc, yo, xe, ter, los, shr, adj, shm, shi, slo, tot,
    ssem, rsem, lsem,
):
    tile = lax.axis_index("tile")
    lev = lax.axis_index("lev")
    core = lev % 2
    chip = lev // 2
    partner = chip * 2 + 1 - core
    across = (lev + 2) % 4
    diagonal = (partner + 2) % 4
    above = (lev + 3) % 4
    nxt = ((tile + 1) % TILES, lev)
    prv = ((tile + TILES - 1) % TILES, lev)
    peers = ((tile, partner), (tile, across), (tile, diagonal))

    bar = pltpu.get_barrier_semaphore()
    for q in peers + (nxt, prv):
        pl.semaphore_signal(bar, inc=1, device_id=q, device_id_type=MESH)

    def remote(i, src, dst, to):
        return pltpu.make_async_remote_copy(
            src_ref=src, dst_ref=dst, send_sem=ssem.at[i], recv_sem=rsem.at[i],
            device_id=to, device_id_type=MESH)

    nat = [pltpu.make_async_copy(s, d, lsem.at[L_NAT + i]) for i, (s, d) in enumerate(((th_ref, tn), (hu_ref, hn)))]
    small = [
        pltpu.make_async_copy(s, d, lsem.at[L_SMALL + i])
        for i, (s, d) in enumerate(((te_ref, ter), (lo_ref, los), (sh_ref, shr), (ad_ref, adj)))
    ]
    fold = []
    for i, (s, d) in enumerate(((th_ref, tf), (hu_ref, hf), (mx_ref, sf))):
        for g in range(8):
            fold.append(
                pltpu.make_async_copy(s.at[:, pl.ds(GRP * g, GRP)], d.at[:, g, :], lsem.at[L_FOLD + 8 * i + g])
            )
    trc = [
        pltpu.make_async_copy(tr_ref.at[n], xa.at[pl.ds(LEV * n, LEV), pl.ds(HALO, COLS)], lsem.at[L_TRC + n])
        for n in range(NTR)
    ]
    for c in nat + fold + small + trc:
        c.start()
    xa[:, pl.ds(0, HALO)] = jnp.zeros((ROWS, HALO), BF)
    xa[:, pl.ds(HALO + COLS, HALO)] = jnp.zeros((ROWS, HALO), BF)

    row = lax.broadcasted_iota(jnp.int32, (48, LEV), 0)
    col = lax.broadcasted_iota(jnp.int32, (48, LEV), 1)
    tri = jnp.where(row >= LEV, 1.0, jnp.where(col > row, 1.0, jnp.where(col == row, 0.5, 0.0))).astype(BF)
    for c in nat:
        c.wait()

    def natural(i, _):
        cs = pl.ds(pl.multiple_of(i * GRP, GRP), GRP)
        v = tn[:, cs] * (1.0 + 0.608 * hn[:, cs])
        vn[:, cs] = v
        v1 = v.astype(BF)
        vb[:, cs] = v1
        rest = v - v1.astype(F32)
        v2 = rest.astype(BF)
        v3 = (rest - v2.astype(F32)).astype(BF)
        part = jnp.dot(tri, v1, preferred_element_type=F32)
        part = part + jnp.dot(tri, v2, preferred_element_type=F32)
        part = part + jnp.dot(tri, v3, preferred_element_type=F32)
        gh[:, cs] = part[:LEV]
        sums[0, :, cs] = part[LEV : LEV + 1]
        return 0

    lax.fori_loop(0, 8, natural, 0)
    for c in fold:
        c.wait()
    for k in range(LEV):
        kap = sf[k] * (tf[k] * (1.0 + 0.608 * hf[k]))
        if k == 0:
            kap = jnp.where(lev == 0, 0.0, kap)
            ktop[...] = kap
        sf[k] = kap

    def step(k, below, e, gg):
        a = sf[k]
        d = 1.0 + a + below
        if k:
            d = d - a * e
        r = 1.0 / d
        p = a * r
        e = below * r
        gg = p * gg if k else p
        rf[k] = r
        pf[k] = p
        ef[k] = e
        gf[k] = gg
        return r, p, e, gg

    e = None
    gg = None
    for k in range(LEV - 1):
        _, _, e, gg = step(k, sf[k + 1], e, gg)
    for c in small:
        c.wait()

    t = [adj[pl.ds(m, 1), :] for m in range(6)]
    s = [shr[pl.ds(m, 1), :] for m in range(6)]
    total = s[0]
    for m in range(1, 6):
        total = total + s[m]
    tot[...] = total
    for m in range(6):
        acc = s[m]
        for q in range(m):
            acc = acc + jnp.where(t[q] == t[m], s[q], 0.0)
        shm[pl.ds(m, 1), :] = acc
    merged = shm[...]
    high = merged.astype(BF)
    shi[...] = high
    slo[...] = (merged - high.astype(F32)).astype(BF)

    ids = lax.broadcasted_iota(jnp.int32, (BLK, BLK), 0).astype(F32).astype(BF)

    def tables(j):
        cs = pl.ds(pl.multiple_of(j * BLK, BLK), BLK)
        place = (adj[:, cs] - j * BLK).astype(F32)
        high = shi[:, cs]
        low = slo[:, cs]
        hs = [jnp.broadcast_to(high[m : m + 1], (BLK, BLK)) for m in range(6)]
        ls = [jnp.broadcast_to(low[m : m + 1], (BLK, BLK)) for m in range(6)]
        return place, hs, ls

    def chunk(tab, offset):
        place, hs, ls = tab
        u = jnp.clip(place - offset, -1.0, float(BLK)).astype(BF)
        hi = jnp.zeros((BLK, BLK), BF)
        lw = jnp.zeros((BLK, BLK), BF)
        for m in range(6):
            hit = jnp.broadcast_to(u[m : m + 1], (BLK, BLK)) == ids
            hi = jnp.where(hit, hs[m], hi)
            lw = jnp.where(hit, ls[m], lw)
        return hi, lw

    def build(tab, w, r):
        hi, lw = chunk(tab, float(BLK * r))
        w[0, pl.ds(BLK * r, BLK), :] = hi
        w[1, pl.ds(BLK * r, BLK), :] = lw

    first = tables(4)
    for r in range(9):
        build(first, w0, r)

    pl.semaphore_wait(bar, 5)
    c_sum = [remote(R_SUM + d, sums.at[0], sums.at[1 + d], peers[d]) for d in range(3)]
    c_kap = remote(R_KAP, ktop, kbot, (tile, above))
    for c in c_sum:
        c.start()
    c_kap.start()
    c_trc = {}
    for i in range(4):
        for d, q, to in ((0, 3 - i, nxt), (1, i, prv)):
            src = tr_ref.at[:, :, pl.ds((COLS - HALO if d == 0 else 0) + BLK * q, BLK)]
            c_trc[d, q] = remote(R_TRC + 4 * d + q, src, xh.at[d, :, :, pl.ds(BLK * q, BLK)], to)
            c_trc[d, q].start()

    c_kap.wait_recv()
    r, p, e, gg = step(LEV - 1, kbot[...], e, gg)
    hh = e
    hfo[LEV - 1] = hh
    cfo[1] = gg
    cfo[3] = hh
    for k in range(LEV - 2, -1, -1):
        e = ef[k]
        gg = gf[k] + e * gg
        hh = e * hh
        gf[k] = gg
        hfo[k] = hh
    cfo[0] = gg
    cfo[2] = hh
    c_cof = remote(R_COF, cfo, cfi, (tile, partner))
    c_cof.start()

    for c in c_sum:
        c.wait_recv()
    peer_levs = (partner, across, diagonal)

    def split(v):
        hi = v.astype(BF)
        return hi, (v - hi.astype(F32)).astype(BF)

    sub16 = lax.broadcasted_iota(jnp.int32, (16, GRP), 0)

    def put_extra(ref, r0, cs, height, stress):
        hi, low = split(height)
        ref[pl.ds(r0, LEV), cs] = hi
        ref[pl.ds(r0 + 48, LEV), cs] = low
        shi_, slo_ = split(stress)
        both = jnp.where(
            sub16 == 0,
            jnp.broadcast_to(shi_.astype(F32), (16, GRP)),
            jnp.where(sub16 == 1, jnp.broadcast_to(slo_.astype(F32), (16, GRP)), 0.0),
        )
        ref[pl.ds(r0 + 32, 16), cs] = both.astype(BF)

    def heights(i, _):
        cs = pl.ds(pl.multiple_of(i * GRP, GRP), GRP)
        below = jnp.zeros((1, GRP), F32)
        for d in range(3):
            below = below + jnp.where(peer_levs[d] > lev, sums[1 + d, :, cs], 0.0)
        base = ter[:, cs] + below / LEVELS
        stress = los[:, cs]
        bl[pl.ds(0, 1), cs] = base
        bl[pl.ds(1, 1), cs] = stress
        height = base + gh[:, cs] / LEVELS
        gh[:, cs] = height
        put_extra(xa, 256, pl.ds(pl.multiple_of(HALO + i * GRP, GRP), GRP), height, stress)
        return 0

    lax.fori_loop(0, 8, heights, 0)
    c_hal = []
    for d, (lo, to) in enumerate(((COLS - HALO, nxt), (0, prv))):
        c_hal.append(remote(R_VIR + d, vb.at[:, pl.ds(lo, HALO)], vh.at[d], to))
        c_hal.append(remote(R_BAS + d, bl.at[:, pl.ds(lo, HALO)], blh.at[d], to))
    for c in c_hal:
        c.start()
    out_gh = pltpu.make_async_copy(gh, gh_out, lsem.at[L_OUT])
    out_gh.start()

    def fused(j, w, todo, lo=0, hi=9):
        parts = [range(q, min(q + PART, hi)) for q in range(lo, hi, PART)]
        share_out = -(-len(todo) // len(parts))
        high = None
        low = None
        for i, part in enumerate(parts):
            for work in todo[share_out * i : share_out * (i + 1)]:
                work()
            at = BLK * part[0]
            n = BLK * len(part)
            xs = pl.ds(pl.multiple_of(BLK * j, BLK) + at, n)
            d = jnp.dot(xa[:, xs], w[0, pl.ds(at, n), :], preferred_element_type=F32)
            high = d if high is None else high + d
            d = jnp.dot(xa[pl.ds(0, 304), xs], w[1, pl.ds(at, n), :], preferred_element_type=F32)
            low = d if low is None else low + d
        cs = pl.ds(pl.multiple_of(j * BLK, BLK), BLK)
        es = pl.ds(pl.multiple_of(HALO + j * BLK, BLK), BLK)
        total = tot[:, cs]
        own = xa[pl.ds(0, 256), es].astype(F32)
        mixed = own * (1.0 - 0.05 * total) + 0.05 * (high[:256] + low[:256])
        mm[2 * j] = mixed[:, :128]
        mm[2 * j + 1] = mixed[:, 128:]
        ends = high[288:290] + low[288:290]
        stress = ends[0:1] + ends[1:2] - los[:, cs] * total
        height = high[256:288] + low[256:288] + high[304:336]
        fo[:, cs] = (height - gh[:, cs] * total) + vn[:, cs] * stress

    def halo_product(c0, n, x):
        ws = pl.ds(BLK * c0, BLK * n)
        return jnp.dot(x, wh[0, ws, :], preferred_element_type=F32) + jnp.dot(
            x, wh[1, ws, :], preferred_element_type=F32
        )

    halo_parts = {}
    at = 0
    for j in range(4):
        halo_parts[j] = (at, 4 - j, 0, BLK * j)
        at += 4 - j
    for j in range(4):
        halo_parts[12 + j] = (at, j + 1, 1, 0)
        at += j + 1

    def own_range(b):
        return (4 - b, 9) if b < 4 else (0, 20 - b)

    def jobs(b, w, skip_own=False):
        tab = tables(b)
        lo, hi = own_range(b)
        c0 = halo_parts[b][0]

        def own(r):
            return lambda: build(tab, w, r)

        def far(i, r):
            def go():
                up, down = chunk(tab, float(BLK * r))
                ws = pl.ds(BLK * (c0 + i), BLK)
                wh[0, ws, :] = up
                wh[1, ws, :] = down

            return go

        beyond = [r for r in range(9) if not lo <= r < hi]
        out = [far(i, r) for i, r in enumerate(beyond)]
        return out if skip_own else [own(r) for r in range(lo, hi)] + out

    for c in trc:
        c.wait()

    def pair(i, _):
        j = 4 + 2 * i
        tab1 = tables(j + 1)
        fused(j, w0, [lambda r=r: build(tab1, w1, r) for r in range(9)])
        tab2 = tables(j + 2)
        fused(j + 1, w1, [lambda r=r: build(tab2, w0, r) for r in range(9)])
        return 0

    lax.fori_loop(0, 4, pair, 0)
    order = (12, 13, 14, 15, 3, 2, 1, 0)
    for i, b in enumerate(order):
        slot, other = (w0, w1) if i % 2 == 0 else (w1, w0)
        todo = jobs(order[i + 1], other) if i < 7 else []
        if i == 0:
            todo = todo + jobs(b, None, True)
        fused(b, slot, todo, *own_range(b))

    def bc(ref, k, g):
        return jnp.broadcast_to(ref[k, pl.ds(g, 1), :], (NTR, GRP))

    def solve(pair_of):
        chains = [(gi, q) for gi in pair_of for q in range(4)]

        def lane(ref, k, c):
            return jnp.broadcast_to(ref[k, pl.ds(c[0], 1), pl.ds(128 * c[1], 128)], (NTR, 128))

        f = [None] * 8
        for k in range(LEV):
            for i, c in enumerate(chains):
                b = 4 * c[0] + c[1]
                v = mm[b, pl.ds(k, NTR, stride=LEV), :] * lane(rf, k, c)
                f[i] = v + lane(pf, k, c) * f[i] if k else v
                yk[b, k] = f[i]
        for i, c in enumerate(chains):
            yb[1, :, pl.ds(c[0] * GRP + 128 * c[1], 128)] = f[i]
        for k in range(LEV - 2, -1, -1):
            for i, c in enumerate(chains):
                b = 4 * c[0] + c[1]
                f[i] = yk[b, k] + lane(ef, k, c) * f[i]
                yk[b, k] = f[i]
        for i, c in enumerate(chains):
            yb[0, :, pl.ds(c[0] * GRP + 128 * c[1], 128)] = f[i]

    def ends(i):
        cs = pl.ds(*SPANS[i])
        return remote(R_YB + i, yb.at[:, :, cs], yp.at[:, :, cs], (tile, partner))

    def chips(i):
        cs = pl.ds(*SPANS[i])
        return remote(R_YC + i, yc.at[:, cs], yo.at[:, cs], (tile, across))

    c_yb = [ends(i) for i in range(5)]
    c_yc = [chips(i) for i in range(5)]

    solve((2, 3))
    solve((4, 5))
    c_yb[0].start()
    runs = ((8, 16), (4, 4), (24, 4), (0, 4), (28, 4))

    def send_y(i):
        first, count = runs[i]

        def one(q, _):
            b = first + q
            ls = pl.ds(pl.multiple_of(b * 128, 128), 128)
            for n in range(NTR):
                pltpu.make_async_copy(yk.at[b, :, n, :], y_out.at[n, :, ls], lsem.at[L_OUT + 19 + i]).start()
            return 0

        lax.fori_loop(0, count, one, 0)

    def wait_y(i):
        first, count = runs[i]
        part = y_out.at[:, :, pl.ds(128 * first, 128 * count)]
        pltpu.make_async_copy(part, part, lsem.at[L_OUT + 19 + i]).wait()

    send_y(0)

    c_cof.wait_recv()
    upper = core == 0

    def pick(i, j):
        return jnp.where(upper, cfo[i], cfi[i]), jnp.where(upper, cfi[j], cfo[j])

    g_bu, g_bl = pick(1, 1)
    g_tu, g_tl = pick(0, 0)
    h_tu, h_tl = pick(2, 2)
    h_bu, h_bl = pick(3, 3)
    dd = 1.0 / (1.0 - g_tl * h_bu)
    mine = jnp.where(chip == 0, h_bl + g_bl * h_bu * dd * h_tl, g_tu + h_tu * dd * g_tl * g_bu)
    cho[...] = mine
    dq[0] = dd
    dq[1] = dd * (g_tl * g_bu + h_tl)
    dq[2] = g_tl
    dq[3] = h_bu
    dq[4] = g_bu
    dq[5] = g_bl
    dq[6] = h_tu
    c_chp = remote(R_CHP, cho, chi, (tile, across))
    c_chp.start()

    def merge(g):
        cs = pl.ds(g * GRP, GRP)
        yt_u = jnp.where(upper, yb[0, :, cs], yp[0, :, cs])
        yb_u = jnp.where(upper, yb[1, :, cs], yp[1, :, cs])
        yt_l = jnp.where(upper, yp[0, :, cs], yb[0, :, cs])
        yb_l = jnp.where(upper, yp[1, :, cs], yb[1, :, cs])
        t0 = bc(dq, 0, g) * (yt_l + bc(dq, 2, g) * yb_u)
        y0 = yb_l + bc(dq, 5, g) * (yb_u + bc(dq, 3, g) * t0)
        y1 = yt_u + bc(dq, 6, g) * t0
        yc[:, cs] = jnp.where(chip == 0, y0, y1)
        xe[0, :, cs] = t0
        xe[1, :, cs] = yb_u

    def finish(g):
        cs = pl.ds(g * GRP, GRP)
        one = pl.ds(g, 1)
        cm = cho[one, :]
        co = chi[one, :]
        scale = jnp.broadcast_to(1.0 / (1.0 - cm * co), (NTR, GRP))
        other = scale * (yo[:, cs] + jnp.broadcast_to(co, (NTR, GRP)) * yc[:, cs])
        t_l = xe[0, :, cs] + bc(dq, 1, g) * other
        b_u = xe[1, :, cs] + bc(dq, 3, g) * t_l + bc(dq, 4, g) * other
        xe[0, :, cs] = jnp.where(upper, other, b_u)
        xe[1, :, cs] = jnp.where(upper, t_l, other)

    out_g = []
    for g in range(8):
        hs = pl.ds(GRP * g, GRP)
        out_g.append(pltpu.make_async_copy(gf.at[:, g, :], g_out.at[:, hs], lsem.at[L_OUT + 1 + g]))
        out_g.append(pltpu.make_async_copy(hfo.at[:, g, :], h_out.at[:, hs], lsem.at[L_OUT + 9 + g]))
    for c in out_g:
        c.start()

    c_yb[0].wait_recv()

    for g in range(2, 6):
        merge(g)
    c_yc[0].start()

    stages = (
        (((0, 3), (1, 0), (0, 2), (1, 1)), (3, 12, 2, 13), (1, 6), (1, 2)),
        (((0, 1), (1, 2), (0, 0), (1, 3)), (1, 14, 0, 15), (0, 7), (3, 4)),
    )

    def join(groups, ids):
        for i in ids:
            c_yb[i].wait_recv()
        for g in groups:
            merge(g)
        for i in ids:
            c_yc[i].start()

    for chunks, blocks, groups, span_ids in stages:
        for key in chunks:
            c_trc[key].wait_recv()
        for b in blocks:
            c0, n, d, x0 = halo_parts[b]
            a = halo_product(c0, n, xh[d, :, :, pl.ds(x0, BLK * n)].reshape(256, BLK * n))
            mm[2 * b] = mm[2 * b] + 0.05 * a[:, :128]
            mm[2 * b + 1] = mm[2 * b + 1] + 0.05 * a[:, 128:]
        solve(groups)
        for i in span_ids:
            c_yb[i].start()
        for i in span_ids:
            send_y(i)
    join(*stages[0][2:])

    join(*stages[1][2:])

    for c in c_hal:
        c.wait_recv()
    for d in range(2):
        for i in range(2):
            cs = pl.ds(GRP * i, GRP)
            part = jnp.dot(tri[:LEV], vh[d, :, cs], preferred_element_type=F32)
            put_extra(xg.at[d], 0, cs, blh[d, pl.ds(0, 1), cs] + part / LEVELS, blh[d, pl.ds(1, 1), cs])
    for b, (c0, n, d, x0) in halo_parts.items():
        a = halo_product(c0, n, xg[d, :, pl.ds(x0, BLK * n)])
        cs = pl.ds(b * BLK, BLK)
        fo[:, cs] = fo[:, cs] + (a[:32] + a[48:80]) + vn[:, cs] * (a[32:33] + a[33:34])
    out_fo = pltpu.make_async_copy(fo, fo_out, lsem.at[L_OUT + 17])
    out_fo.start()

    c_chp.wait_recv()
    for c in c_yc:
        c.wait_recv()

    for g in range(8):
        finish(g)
    out_e = pltpu.make_async_copy(xe, ends_out, lsem.at[L_OUT + 18])
    out_e.start()

    for c in c_sum + [c_kap, c_cof, c_chp] + list(c_trc.values()) + c_hal + c_yb + c_yc:
        c.wait_send()
    for c in [out_gh] + out_g + [out_fo, out_e]:
        c.wait()
    for i in range(5):
        wait_y(i)


def combine(y_ref, e_ref, g_ref, h_ref, gh_ref, fo_ref, gh_out, fo_out, x_out):
    g = g_ref[...]
    h = h_ref[...]
    for n in range(NTR):
        x_out[n] = y_ref[n] + g * e_ref[0, pl.ds(n, 1), :] + h * e_ref[1, pl.ds(n, 1), :]
    gh_out[...] = gh_ref[...]
    fo_out[...] = fo_ref[...]


def local(thermal, humid, mixing, tracers, terrain, stress, share, table):
    f32 = lambda *s: jax.ShapeDtypeStruct(s, F32)
    vm = lambda *s: pltpu.VMEM(s, F32)
    vb = lambda *s: pltpu.VMEM(s, BF)
    fold = vm(LEV, 8, GRP)
    nat = vm(LEV, COLS)
    anyspec = pl.BlockSpec(memory_space=pl.ANY)
    y, ends, g, h, gh, fo = pl.pallas_call(
        kernel,
        out_shape=(f32(NTR, LEV, COLS), f32(2, NTR, COLS), f32(LEV, COLS), f32(LEV, COLS), f32(LEV, COLS), f32(LEV, COLS)),
        in_specs=[pl.BlockSpec(memory_space=pltpu.HBM)] * 8,
        out_specs=(anyspec,) * 6,
        scratch_shapes=[
            vb(ROWS, EXT), vb(2, NTR, LEV, HALO), vb(2, 80, HALO), vb(2, WIN, BLK), vb(2, WIN, BLK), vb(2, 20 * BLK, BLK),
            vm(32, 256, 128), vm(32, LEV, NTR, 128), nat, nat, nat, nat, nat, fold, fold, fold,
            fold, fold, fold, fold, fold, vm(4, 1, COLS), vm(8, GRP), vm(8, GRP),
            vb(LEV, COLS), vb(2, LEV, HALO), vm(2, COLS), vm(2, 2, HALO),
            vm(4, 8, GRP), vm(4, 8, GRP), vm(8, GRP), vm(8, GRP), vm(7, 8, GRP),
            vm(2, NTR, COLS), vm(2, NTR, COLS), vm(NTR, COLS), vm(NTR, COLS), vm(2, NTR, COLS),
            vm(1, COLS), vm(1, COLS), vm(6, COLS), pltpu.VMEM((6, COLS), jnp.int32),
            vm(6, COLS), vb(6, COLS), vb(6, COLS), vm(1, COLS),
            pltpu.SemaphoreType.DMA((N_REMOTE,)), pltpu.SemaphoreType.DMA((N_REMOTE,)),
            pltpu.SemaphoreType.DMA((N_LOCAL + N_OUT,)),
        ],
        compiler_params=pltpu.CompilerParams(collective_id=0, has_side_effects=True, vmem_limit_bytes=39 << 20),
        name="band",
    )(*[pltpu.with_memory_space_constraint(v, pltpu.HBM) for v in (thermal, humid, mixing, tracers, terrain[None], stress[None], share, table)])
    width = 1024
    full = lambda *lead: pl.BlockSpec(lead + (width,), lambda i: (0,) * len(lead) + (i,))
    gh2, fo2, x = pl.pallas_call(
        combine,
        grid=(COLS // width,),
        out_shape=(f32(LEV, COLS), f32(LEV, COLS), f32(NTR, LEV, COLS)),
        in_specs=[full(NTR, LEV), full(2, NTR), full(LEV), full(LEV), full(LEV), full(LEV)],
        out_specs=(full(LEV), full(LEV), full(NTR, LEV)),
        compiler_params=pltpu.CompilerParams(vmem_limit_bytes=14 << 20),
        name="combine",
    )(y, ends, g, h, gh, fo)
    return gh2, fo2, x


def solution(mesh):
    return jax.shard_map(
        local,
        mesh=mesh,
        in_specs=(
            P("lev", "tile"), P("lev", "tile"), P("lev", "tile"), P(None, "lev", "tile"),
            P("tile"), P("tile"), P(None, "tile"), P(None, "tile"),
        ),
        out_specs=(P("lev", "tile"), P("lev", "tile"), P(None, "lev", "tile")),
        check_vma=False,
    )
```
